32 devices in a mesh: pipe: 4 (over y, x), ctx: 8 (over z, core).
Axes of the slice: x: 2, y: 2, z: 4, core: 2. Of those that a mesh axis runs over, the one named last changes fastest.
Arguments:
- queries: bfloat16 [4, 1024, 3072], P('pipe', 'ctx'), may hold values from -40 to 40
- keys: bfloat16 [4, 1024, 3072], P('pipe', 'ctx'), may hold values from -6 to 6
- values: bfloat16 [4, 1024, 3072], P('pipe', 'ctx'), may hold values from -6 to 6
- residual: bfloat16 [4, 1024, 3072], P('pipe', 'ctx'), may hold values from -6 to 6
- gate: float32 [4, 3072], P('pipe'), may hold values from 0.5 to 2
- tile_lists: int32 [4, 8, 24, 5], P('pipe', 'ctx'), may hold values from 0 to 7, as said below
- counts: int32 [4, 8, 24], P('pipe', 'ctx'), may hold values from 1 to 5
Outputs:
- passed: bfloat16 [4, 1024, 3072], P('pipe', 'ctx')
The draws below stay inside these ranges and needn't reach their ends.
Inputs may be any that keep to these rules, and one draw needn't show every extreme that they name: `tile_lists`: each list names 5 distinct tiles, none equal to its query tile; entries past the count are tiles too. Over the 24 lists of one query tile no tile is named more than 18 times, and some tile is named exactly 18 times.
All inputs are finite; a program needn't handle non-finite values.
Results may differ from the reference program's by a relative error of at most 0.0022.
Values may be sent and summed in bfloat16 or wider, within the bound.
No kernel may reach another device: no remote copies, remote signals or barrier semaphores. Data moves between devices by JAX's collectives and lax.ppermute only.
A program may use at most 128 MiB of HBM per device.

```python
import math
import jax
import jax.numpy as jnp
from jax import lax

HEADS = 24
HEAD_DIM = 128
D = 3072
TILE = 128
K_LIST = 5
SECTIONS = 4
TILES = 8
TOKENS = 1024


def query_key_pair(key):
    base = jax.random.fold_in(key, 4711)
    query_key, key_key = jax.random.split(base, 2)
    shape = (SECTIONS, TOKENS, D)
    key_vals = jnp.clip(jax.random.normal(key_key, shape, jnp.float32), -6.0, 6.0)
    query_vals = jnp.clip(jax.random.normal(query_key, shape, jnp.float32), -6.0, 6.0)
    return (query_vals, key_vals)


def draw_queries(key, part):
    return query_key_pair(key)[0].astype(jnp.bfloat16)


def draw_keys(key, part):
    return query_key_pair(key)[1].astype(jnp.bfloat16)


def draw_tile_lists(key, part):
    base = jax.random.fold_in(key, 917)
    span = TILES - 1
    all_keys = jax.random.split(base, SECTIONS * TILES)
    orders = jax.vmap(lambda single: jax.random.permutation(single, span))(all_keys)
    orders = orders.reshape(SECTIONS, TILES, span).astype(jnp.int32)
    spots = jnp.arange(HEADS * K_LIST, dtype=jnp.int32) % span
    offsets = 1 + orders[:, :, spots]
    query_tile = jnp.arange(TILES, dtype=jnp.int32)[None, :, None]
    return ((query_tile + offsets) % TILES).reshape(SECTIONS, TILES, HEADS, K_LIST).astype(jnp.int32)


def with_ends(result, stream_key, smallest, largest):
    index_at = [jax.random.randint(jax.random.fold_in(stream_key, axis), (), 0, length) for axis, length in enumerate(result.shape)]
    widest = result.shape.index(max(result.shape))
    neighbour = index_at[:widest] + [(index_at[widest] + 1) % result.shape[widest]] + index_at[widest + 1:]
    return result.at[tuple(index_at)].set(smallest).at[tuple(neighbour)].set(largest)


def block_scale(stream_key, extent, cuts, low, largest):
    def one(dim, parts):
        heights = jax.random.uniform(jax.random.fold_in(jax.random.fold_in(stream_key, 6), dim), (parts,), jnp.float32, low / len(cuts), largest / len(cuts))
        return jnp.repeat(jnp.exp(heights), extent[dim] // parts).reshape((-1,) + (1,) * (len(extent) - dim - 1))

    factor_of = one(*cuts[0])
    for cut in cuts[1:]:
        factor_of = factor_of * one(*cut)
    return factor_of


def centred(stream_key, shape, deviation, most, cuts=(), kind=jnp.bfloat16):
    level = block_scale(stream_key, shape, cuts, -0.22, 0.18) if cuts else 1.0
    result = jax.random.normal(stream_key, shape, jnp.float32) * deviation * level
    return jnp.minimum(jnp.maximum(result, -most), most).astype(kind)


def setup_inputs(seed: int = 0) -> dict:
    splits = jax.random.split(jax.random.key(seed), 8)
    return {
        "queries": draw_queries(jax.random.fold_in(splits[7], 71), 0),
        "keys": draw_keys(jax.random.fold_in(splits[7], 71), 0),
        "values": centred(splits[2], (SECTIONS, TOKENS, D), 1.0, 6.0, ((0, 4), (1, 8))),
        "residual": centred(splits[3], (SECTIONS, TOKENS, D), 1.0, 6.0, ((0, 4), (1, 8))),
        "gate": jnp.clip(0.5 + 1.5 * jax.random.uniform(splits[4], (SECTIONS, D), jnp.float32) ** block_scale(splits[4], (SECTIONS, D), ((0, 4),), -0.2, 0.2), 0.5, 2.0),
        "tile_lists": draw_tile_lists(jax.random.fold_in(splits[7], 71), 0),
        "counts": with_ends(jax.random.randint(splits[6], (SECTIONS, TILES, HEADS), 1, K_LIST + 1), jax.random.fold_in(splits[6], 1), 1, K_LIST).astype(jnp.int32),
    }


def tile_attention(qi, near_k, near_v, near_ok, far_k, far_v, far_ok):
    scale = 1.0 / math.sqrt(HEAD_DIM)
    local = jnp.einsum('hqd,hjd->hqj', qi, near_k) * scale
    remote = jnp.einsum('hqd,hjd->hqj', qi, far_k) * scale
    local_ok = near_ok[None, None, :]
    remote_ok = far_ok[:, None, :]
    top = jnp.maximum(lax.optimization_barrier(jnp.max(jnp.where(local_ok, local, -1e+30), axis=-1, keepdims=True)), lax.optimization_barrier(jnp.max(jnp.where(remote_ok, remote, -1e+30), axis=-1, keepdims=True)))
    p_local = jnp.where(local_ok, jnp.exp(local - top), 0.0)
    p_far = jnp.where(remote_ok, jnp.exp(remote - top), 0.0)
    total = lax.optimization_barrier(jnp.sum(p_local, axis=-1, keepdims=True)) + lax.optimization_barrier(jnp.sum(p_far, axis=-1, keepdims=True))
    r_local = lax.optimization_barrier(p_local.astype(jnp.bfloat16)).astype(jnp.float32)
    r_far = lax.optimization_barrier(p_far.astype(jnp.bfloat16)).astype(jnp.float32)
    mixed = jnp.einsum('hqj,hjd->hqd', r_local, near_v) + jnp.einsum('hqj,hjd->hqd', r_far, far_v)
    return mixed / total

def reference(queries, keys, values, residual, gate, tile_lists, counts):

    def one_section(inputs):
        query_rows, key_rows, value_rows, resid, gain, lists, valid = inputs
        key_tiles = key_rows.reshape(TILES, TILE, HEADS, HEAD_DIM).transpose(2, 0, 1, 3)
        value_tiles = value_rows.reshape(TILES, TILE, HEADS, HEAD_DIM).transpose(2, 0, 1, 3)
        query_tiles = query_rows.reshape(TILES, TILE, HEADS, HEAD_DIM)
        head_ids = jnp.arange(HEADS, dtype=jnp.int32)[:, None]

        def one_tile(index):
            qi = query_tiles[index].transpose(1, 0, 2).astype(jnp.float32)
            near_idx = jnp.clip(index + jnp.arange(3, dtype=jnp.int32) - 1, 0, TILES - 1).astype(jnp.int32)
            near_k = key_tiles[:, near_idx].reshape(HEADS, 3 * TILE, HEAD_DIM).astype(jnp.float32)
            near_v = value_tiles[:, near_idx].reshape(HEADS, 3 * TILE, HEAD_DIM).astype(jnp.float32)
            near_ok = jnp.repeat(jnp.stack([index > 0, index >= 0, index < TILES - 1]), TILE)
            chosen = lists[index].astype(jnp.int32)
            far_k = key_tiles[head_ids, chosen].reshape(HEADS, K_LIST * TILE, HEAD_DIM).astype(jnp.float32)
            far_v = value_tiles[head_ids, chosen].reshape(HEADS, K_LIST * TILE, HEAD_DIM).astype(jnp.float32)
            far_ok = jnp.repeat(jnp.arange(K_LIST, dtype=jnp.int32)[None, :] < valid[index][:, None], TILE, axis=1)
            return tile_attention(qi, near_k, near_v, near_ok, far_k, far_v, far_ok)
        heads_out = lax.map(one_tile, jnp.arange(TILES, dtype=jnp.int32))
        attention = heads_out.transpose(0, 2, 1, 3).reshape(TOKENS, D)
        return (resid.astype(jnp.float32) + gain[None, :] * attention).astype(jnp.bfloat16)
    updated = lax.map(one_section, (queries, keys, values, residual, gate, tile_lists, counts))
    return jnp.roll(updated, 1, axis=0)
```

```python
import functools
import math

import jax
import jax.numpy as jnp
from jax import lax
from jax.experimental import pallas as pl
from jax.experimental.pallas import tpu as pltpu
from jax.sharding import PartitionSpec as P

HEADS = 24
HEAD_DIM = 128
K_LIST = 5
SCALE = math.log2(math.e) / math.sqrt(HEAD_DIM)
MASKED = -1e30


def dot_nt(a, b):
    return lax.dot_general(a, b, (((1,), (1,)), ((), ())), preferred_element_type=jnp.float32)


def attend(query, key_tiles, value_tiles, mults):
    scores = []
    top = None
    for key, mult in zip(key_tiles, mults):
        bias = jnp.where(mult > 0, 0.0, MASKED)
        one = dot_nt(query, key) * SCALE + bias
        scores.append(one)
        peak = jnp.max(one, axis=-1, keepdims=True)
        top = peak if top is None else jnp.maximum(top, peak)
    total = None
    mixed = None
    for one, value, mult in zip(scores, value_tiles, mults):
        weights = jnp.exp2(one - top) * mult
        part = jnp.sum(weights, axis=-1, keepdims=True)
        moved = jnp.dot(weights.astype(jnp.bfloat16), value, preferred_element_type=jnp.float32)
        total = part if total is None else total + part
        mixed = moved if mixed is None else mixed + moved
    return mixed / total


def finish(residual, gate, attention):
    return (residual.astype(jnp.float32) + gate * attention).astype(jnp.bfloat16)


def dense_kernel(tiles, mult_ref, q_ref, k_ref, v_ref, r_ref, g_ref, o_ref):
    head = pl.program_id(0)
    rows = q_ref.shape[0]
    keys = [k_ref[j * rows : (j + 1) * rows, :] for j in range(tiles)]
    vals = [v_ref[j * rows : (j + 1) * rows, :] for j in range(tiles)]
    mults = [mult_ref[head * tiles + j] for j in range(tiles)]
    o_ref[...] = finish(r_ref[...], g_ref[...], attend(q_ref[...], keys, vals, mults))


def multiplicity(lists, valid, me, tiles):
    tile = jnp.arange(tiles)
    near = (jnp.abs(tile - me) <= 1).astype(jnp.int32)
    chosen = (lists[:, :, None] == tile[None, None, :]) & (
        jnp.arange(K_LIST)[None, :] < valid[:, None]
    )[:, :, None]
    return (near[None, :] + jnp.sum(chosen.astype(jnp.int32), axis=1)).astype(jnp.float32)


def shifted(block, axis, distance):
    devices = range(lax.axis_size(axis))
    return lax.ppermute(block, axis, [((i - distance) % len(devices), i) for i in devices])


def gathered_section(queries, keys, values, residual, gate, tile_lists, counts):
    rows = queries.shape[1]
    tiles = lax.axis_size("ctx")
    me = lax.axis_index("ctx")
    all_k = lax.all_gather(keys[0], "ctx", axis=0, tiled=True)
    all_v = lax.all_gather(values[0], "ctx", axis=0, tiled=True)
    mult = multiplicity(tile_lists[0, 0], counts[0, 0], me, tiles).reshape(HEADS * tiles)
    own = pl.BlockSpec((rows, HEAD_DIM), lambda h, m: (0, h))
    full = pl.BlockSpec((tiles * rows, HEAD_DIM), lambda h, m: (0, h))
    updated = pl.pallas_call(
        functools.partial(dense_kernel, tiles),
        out_shape=jax.ShapeDtypeStruct((rows, HEADS * HEAD_DIM), jnp.bfloat16),
        grid_spec=pltpu.PrefetchScalarGridSpec(
            num_scalar_prefetch=1,
            grid=(HEADS,),
            in_specs=[own, full, full, own, pl.BlockSpec((1, HEAD_DIM), lambda h, m: (0, h))],
            out_specs=own,
        ),
    )(mult, queries[0], all_k, all_v, residual[0], gate)
    return shifted(updated[None], "pipe", 1)


def pick_kernel(head_ref, k_ref, v_ref, o_ref):
    o_ref[0, :, :HEAD_DIM] = k_ref[...]
    o_ref[0, :, HEAD_DIM:] = v_ref[...]


def listed_kernel(pick_ref, valid_ref, edge_ref, q_ref, *refs):
    near_k, near_v, far = refs[:3], refs[3:6], refs[6 : 6 + K_LIST]
    r_ref, g_ref, o_ref = refs[6 + K_LIST :]
    head = pl.program_id(0)
    one = jnp.float32(1.0)
    mults = [edge_ref[0].astype(jnp.float32), one, edge_ref[1].astype(jnp.float32)]
    mults += [jnp.where(k < valid_ref[head], 1.0, 0.0) for k in range(K_LIST)]
    keys = [ref[...] for ref in near_k] + [ref[0, :, :HEAD_DIM] for ref in far]
    vals = [ref[...] for ref in near_v] + [ref[0, :, HEAD_DIM:] for ref in far]
    o_ref[...] = finish(r_ref[...], g_ref[...], attend(q_ref[...], keys, vals, mults))


def listed_section(queries, keys, values, residual, gate, tile_lists, counts):
    rows = queries.shape[1]
    tiles = lax.axis_size("ctx")
    me = lax.axis_index("ctx")
    cap = (HEADS * K_LIST + tiles - 2) // (tiles - 1)
    lists = tile_lists[0, 0]
    up = [(i, i + 1) for i in range(tiles - 1)]
    down = [(j, i) for i, j in up]
    near_k = [lax.ppermute(keys[0], "ctx", up), keys[0], lax.ppermute(keys[0], "ctx", down)]
    near_v = [lax.ppermute(values[0], "ctx", up), values[0], lax.ppermute(values[0], "ctx", down)]
    flat = lax.all_gather(lists.reshape(1, HEADS * K_LIST), "ctx", axis=0, tiled=True)

    def entry_ranks(entries):
        same = entries[:, None] == entries[None, :]
        earlier = entry[None, :] < entry[:, None]
        return jnp.sum((same & earlier).astype(jnp.int32), axis=-1)

    mine = flat == me
    entry = jnp.arange(HEADS * K_LIST)
    before = (entry[:, None] < entry[None, :]).astype(jnp.float32)
    rank = jnp.dot(mine.astype(jnp.float32), before).astype(jnp.int32)
    head_of = jnp.arange(HEADS * K_LIST) // K_LIST
    slot = jnp.arange(cap)
    hit = mine[:, :, None] & (rank[:, :, None] == slot[None, None, :])
    heads = jnp.sum(jnp.where(hit, head_of[None, :, None], 0), axis=1).reshape(tiles * cap)
    pair = pl.BlockSpec((rows, HEAD_DIM), lambda i, h: (0, h[i]))
    outgoing = pl.pallas_call(
        pick_kernel,
        out_shape=jax.ShapeDtypeStruct((tiles * cap, rows, 2 * HEAD_DIM), jnp.bfloat16),
        grid_spec=pltpu.PrefetchScalarGridSpec(
            num_scalar_prefetch=1,
            grid=(tiles * cap,),
            in_specs=[pair, pair],
            out_specs=pl.BlockSpec((1, rows, 2 * HEAD_DIM), lambda i, h: (i, 0, 0)),
        ),
    )(heads, keys[0], values[0])
    arrived = lax.all_to_all(outgoing, "ctx", split_axis=0, concat_axis=0, tiled=True)
    own_entries = lists.reshape(HEADS * K_LIST)
    pick = own_entries * cap + entry_ranks(own_entries)
    edge = jnp.stack([me > 0, me < tiles - 1]).astype(jnp.int32)
    own = pl.BlockSpec((rows, HEAD_DIM), lambda h, p, c, e: (0, h))
    far = [
        pl.BlockSpec((1, rows, 2 * HEAD_DIM), lambda h, p, c, e, k=k: (p[h * K_LIST + k], 0, 0))
        for k in range(K_LIST)
    ]
    updated = pl.pallas_call(
        listed_kernel,
        out_shape=jax.ShapeDtypeStruct((rows, HEADS * HEAD_DIM), jnp.bfloat16),
        grid_spec=pltpu.PrefetchScalarGridSpec(
            num_scalar_prefetch=3,
            grid=(HEADS,),
            in_specs=[own] * 7 + far + [own, pl.BlockSpec((1, HEAD_DIM), lambda h, p, c, e: (0, h))],
            out_specs=own,
        ),
    )(pick, counts[0, 0], edge, queries[0], *near_k, *near_v, *([arrived] * K_LIST), residual[0], gate)
    return shifted(updated[None], "pipe", 1)


def solution(mesh):
    rows = P("pipe", "ctx", None)
    placed = (rows, rows, rows, rows, P("pipe", None), P("pipe", "ctx", None, None), rows)
    section = gathered_section if mesh.shape["ctx"] <= 8 else listed_section
    return jax.shard_map(section, mesh=mesh, in_specs=placed, out_specs=rows, check_vma=False)
```

```python
import functools
import math

import jax
import jax.numpy as jnp
from jax import lax
from jax.experimental import pallas as pl
from jax.experimental.pallas import tpu as pltpu
from jax.sharding import PartitionSpec as P

HEADS = 24
HEAD_DIM = 128
K_LIST = 5
GROUPS = (5, 5, 2)
SCALE = math.log2(math.e) / math.sqrt(HEAD_DIM)
MASKED = -1e30


def dot_nt(a, b):
    return lax.dot_general(a, b, (((1,), (1,)), ((), ())), preferred_element_type=jnp.float32)


def attend(query, key_tiles, value_tiles, mults):
    scores = [
        dot_nt(query, key) * SCALE + jnp.where(mult > 0, 0.0, MASKED)
        for key, mult in zip(key_tiles, mults)
    ]
    top = jnp.max(functools.reduce(jnp.maximum, scores), axis=-1, keepdims=True)
    weights = [jnp.exp2(one - top) * mult for one, mult in zip(scores, mults)]
    total = jnp.sum(functools.reduce(jnp.add, weights), axis=-1, keepdims=True)
    rounded = jnp.concatenate([one.astype(jnp.bfloat16) for one in weights], axis=1)
    value = jnp.concatenate(value_tiles, axis=0)
    return jnp.dot(rounded, value, preferred_element_type=jnp.float32) / total


def finish(residual, gate, attention):
    return (residual.astype(jnp.float32) + gate * attention).astype(jnp.bfloat16)


def relay_kernel(first, heads, mult_ref, *refs):
    pairs, rests, (g_ref,), outs = refs[:4], refs[4:6], refs[6:7], refs[7:]
    head = first + pl.program_id(0)
    rows = pairs[0].shape[0] // 4
    tile = [slice(j * rows, (j + 1) * rows) for j in range(4)]
    keys = [ref[tile[j], :] for ref in pairs for j in (0, 2)]
    vals = [ref[tile[j], :] for ref in pairs for j in (1, 3)]
    for t, o_ref in enumerate(outs):
        rest, place = rests[t // 2], 2 * (t % 2)
        mults = [mult_ref[(t * heads + head) * 8 + j] for j in range(8)]
        mixed = attend(rest[tile[place], :], keys, vals, mults)
        o_ref[...] = finish(rest[tile[place + 1], :], g_ref[...], mixed)


def multiplicity(lists, valid, me, tiles):
    tile = jnp.arange(tiles)
    near = (jnp.abs(tile - me) <= 1).astype(jnp.int32)
    chosen = (lists[:, :, None] == tile[None, None, :]) & (
        jnp.arange(K_LIST)[None, :] < valid[:, None]
    )[:, :, None]
    return (near[None, :] + jnp.sum(chosen.astype(jnp.int32), axis=1)).astype(jnp.float32)


def shifted(block, axis, distance):
    devices = range(lax.axis_size(axis))
    return lax.ppermute(block, axis, [((i - distance) % len(devices), i) for i in devices])


def relay_section(queries, keys, values, residual, gate, tile_lists, counts):
    rows = queries.shape[1]
    tiles = lax.axis_size("ctx")
    sections = lax.axis_size("pipe")
    me = lax.axis_index("ctx")
    chip, core = me // 2, me % 2
    half = HEADS // 2
    width = half * HEAD_DIM

    swap = [(i, i ^ 1) for i in range(8)]
    inward = [(2 * z + c, 2 * (z ^ 1) + c) for z in range(4) for c in (0, 1)]
    across = [(2, 4), (3, 5), (4, 2), (5, 3), (0, 1), (1, 0), (6, 7), (7, 6)]

    def onward(change):
        return [
            (p * tiles + i, (p + 1) % sections * tiles + (i ^ change))
            for p in range(sections)
            for i in range(tiles)
        ]

    def ctx(block, route):
        return lax.ppermute(block, "ctx", route)

    def halves(block):
        left, right = block[..., :width], block[..., width:]
        return jnp.where(core == 0, left, right), jnp.where(core == 0, right, left)

    edges = [0]
    for size in GROUPS:
        edges.append(edges[-1] + size)
    cut = [slice(a * HEAD_DIM, b * HEAD_DIM) for a, b in zip(edges, edges[1:])]
    groups = range(len(GROUPS))

    kv_mine, kv_theirs = halves(jnp.concatenate([keys[0], values[0]], axis=0))
    qr_mine, qr_theirs = halves(jnp.concatenate([queries[0], residual[0]], axis=0))
    first = ctx(kv_theirs[:, cut[0]], swap)
    later = ctx(jnp.concatenate([kv_theirs[:, cut[0].stop :], qr_theirs], axis=1), swap)
    kv_got = jnp.concatenate([first, later[:, : width - cut[0].stop]], axis=1)
    qr_got = later[:, width - cut[0].stop :]
    own = [jnp.concatenate([kv_mine[:, c], kv_got[:, c]], axis=0) for c in cut]
    own_qr = [jnp.concatenate([qr_mine[:, c], qr_got[:, c]], axis=0) for c in cut]

    end, end_qr, near, far = [], [], [], []
    for g in groups:
        near.append(ctx(own[g], across))
        end.append(ctx(own[g], inward))
        end_qr.append(ctx(own_qr[g], inward))
        far.append(ctx(end[g], across))

    table = multiplicity(tile_lists[0, 0], counts[0, 0], me, tiles).reshape(2, half, tiles)
    table_mine = jnp.where(core == 0, table[0], table[1])
    table_theirs = jnp.where(core == 0, table[1], table[0])
    table = jnp.stack([table_mine, ctx(table_theirs, swap)])
    table = jnp.concatenate([table, ctx(table, inward)], axis=0)
    chips = jnp.stack([chip, chip ^ 1, 3 - chip, 3 - (chip ^ 1)])
    order = (2 * chips[:, None] + jnp.stack([core, 1 - core])[None, :]).reshape(1, 1, 8, 1)
    table = jnp.sum(jnp.where(order == jnp.arange(tiles), table[:, :, None, :], 0.0), axis=-1)
    table = table.reshape(4 * half * tiles)
    gate_mine, _ = halves(gate)

    block = pl.BlockSpec((4 * rows, HEAD_DIM), lambda h, m: (0, h))
    line = pl.BlockSpec((1, HEAD_DIM), lambda h, m: (0, h))
    one = pl.BlockSpec((rows, HEAD_DIM), lambda h, m: (0, h))
    same, other = [], []
    for g in groups:
        size = GROUPS[g]
        results = pl.pallas_call(
            functools.partial(relay_kernel, edges[g], half),
            out_shape=[jax.ShapeDtypeStruct((rows, size * HEAD_DIM), jnp.bfloat16)] * 4,
            grid_spec=pltpu.PrefetchScalarGridSpec(
                num_scalar_prefetch=1,
                grid=(size,),
                in_specs=[block] * 6 + [line],
                out_specs=[one] * 4,
            ),
            cost_estimate=pl.CostEstimate(
                flops=size * 16 * rows * 8 * rows * HEAD_DIM,
                bytes_accessed=size * 28 * rows * HEAD_DIM * 2,
                transcendentals=size * 4 * rows * 8 * rows,
            ),
        )(table, own[g], end[g], near[g], far[g], own_qr[g], end_qr[g], gate_mine[:, cut[g]])
        sent = [
            lax.ppermute(piece, ("pipe", "ctx"), onward(change))
            for piece, change in zip(results, (0, 1, 2, 3))
        ]
        inner = (chip == 1) | (chip == 2)
        same.append(jnp.where(inner, sent[0], sent[2]))
        other.append(jnp.where(inner, sent[1], sent[3]))
    same, other = jnp.concatenate(same, axis=1), jnp.concatenate(other, axis=1)
    left, right = jnp.where(core == 0, same, other), jnp.where(core == 0, other, same)
    return jnp.concatenate([left, right], axis=1)[None]


def pick_kernel(head_ref, k_ref, v_ref, o_ref):
    o_ref[0, :, :HEAD_DIM] = k_ref[...]
    o_ref[0, :, HEAD_DIM:] = v_ref[...]


def listed_kernel(pick_ref, valid_ref, edge_ref, q_ref, *refs):
    near_k, near_v, far = refs[:3], refs[3:6], refs[6 : 6 + K_LIST]
    r_ref, g_ref, o_ref = refs[6 + K_LIST :]
    head = pl.program_id(0)
    one = jnp.float32(1.0)
    mults = [edge_ref[0].astype(jnp.float32), one, edge_ref[1].astype(jnp.float32)]
    mults += [jnp.where(k < valid_ref[head], 1.0, 0.0) for k in range(K_LIST)]
    keys = [ref[...] for ref in near_k] + [ref[0, :, :HEAD_DIM] for ref in far]
    vals = [ref[...] for ref in near_v] + [ref[0, :, HEAD_DIM:] for ref in far]
    o_ref[...] = finish(r_ref[...], g_ref[...], attend(q_ref[...], keys, vals, mults))


def listed_section(queries, keys, values, residual, gate, tile_lists, counts):
    rows = queries.shape[1]
    tiles = lax.axis_size("ctx")
    me = lax.axis_index("ctx")
    cap = (HEADS * K_LIST + tiles - 2) // (tiles - 1)
    lists = tile_lists[0, 0]
    up = [(i, i + 1) for i in range(tiles - 1)]
    down = [(j, i) for i, j in up]
    near_k = [lax.ppermute(keys[0], "ctx", up), keys[0], lax.ppermute(keys[0], "ctx", down)]
    near_v = [lax.ppermute(values[0], "ctx", up), values[0], lax.ppermute(values[0], "ctx", down)]
    flat = lax.all_gather(lists.reshape(1, HEADS * K_LIST), "ctx", axis=0, tiled=True)

    def entry_ranks(entries):
        same = entries[:, None] == entries[None, :]
        earlier = entry[None, :] < entry[:, None]
        return jnp.sum((same & earlier).astype(jnp.int32), axis=-1)

    mine = flat == me
    entry = jnp.arange(HEADS * K_LIST)
    before = (entry[:, None] < entry[None, :]).astype(jnp.float32)
    rank = jnp.dot(mine.astype(jnp.float32), before).astype(jnp.int32)
    head_of = jnp.arange(HEADS * K_LIST) // K_LIST
    slot = jnp.arange(cap)
    hit = mine[:, :, None] & (rank[:, :, None] == slot[None, None, :])
    heads = jnp.sum(jnp.where(hit, head_of[None, :, None], 0), axis=1).reshape(tiles * cap)
    pair = pl.BlockSpec((rows, HEAD_DIM), lambda i, h: (0, h[i]))
    outgoing = pl.pallas_call(
        pick_kernel,
        out_shape=jax.ShapeDtypeStruct((tiles * cap, rows, 2 * HEAD_DIM), jnp.bfloat16),
        grid_spec=pltpu.PrefetchScalarGridSpec(
            num_scalar_prefetch=1,
            grid=(tiles * cap,),
            in_specs=[pair, pair],
            out_specs=pl.BlockSpec((1, rows, 2 * HEAD_DIM), lambda i, h: (i, 0, 0)),
        ),
    )(heads, keys[0], values[0])
    arrived = lax.all_to_all(outgoing, "ctx", split_axis=0, concat_axis=0, tiled=True)
    own_entries = lists.reshape(HEADS * K_LIST)
    pick = own_entries * cap + entry_ranks(own_entries)
    edge = jnp.stack([me > 0, me < tiles - 1]).astype(jnp.int32)
    own = pl.BlockSpec((rows, HEAD_DIM), lambda h, p, c, e: (0, h))
    far = [
        pl.BlockSpec((1, rows, 2 * HEAD_DIM), lambda h, p, c, e, k=k: (p[h * K_LIST + k], 0, 0))
        for k in range(K_LIST)
    ]
    updated = pl.pallas_call(
        listed_kernel,
        out_shape=jax.ShapeDtypeStruct((rows, HEADS * HEAD_DIM), jnp.bfloat16),
        grid_spec=pltpu.PrefetchScalarGridSpec(
            num_scalar_prefetch=3,
            grid=(HEADS,),
            in_specs=[own] * 7 + far + [own, pl.BlockSpec((1, HEAD_DIM), lambda h, p, c, e: (0, h))],
            out_specs=own,
        ),
    )(pick, counts[0, 0], edge, queries[0], *near_k, *near_v, *([arrived] * K_LIST), residual[0], gate)
    return shifted(updated[None], "pipe", 1)


def solution(mesh):
    rows = P("pipe", "ctx", None)
    placed = (rows, rows, rows, rows, P("pipe", None), P("pipe", "ctx", None, None), rows)
    section = relay_section if mesh.shape["ctx"] == 8 else listed_section
    return jax.shard_map(section, mesh=mesh, in_specs=placed, out_specs=rows, check_vma=False)
```

```python
import functools
import math

import jax
import jax.numpy as jnp
from jax import lax
from jax.experimental import pallas as pl
from jax.experimental.pallas import tpu as pltpu
from jax.sharding import PartitionSpec as P

HEADS = 24
HEAD_DIM = 128
K_LIST = 5
GROUPS = (6, 4, 2)
BLOCKS = (3, 4, 2)
COST = 96
SCALE = math.log2(math.e) / math.sqrt(HEAD_DIM)
MASKED = -1e30


def dot_nt(a, b):
    return lax.dot_general(a, b, (((1,), (1,)), ((), ())), preferred_element_type=jnp.float32)


def attend(query, key, value, mults):
    scores = dot_nt(query, key)
    rows = query.shape[0] // len(mults)
    span = key.shape[0] // len(mults[0])
    rounded, totals = [], []
    for t, counted in enumerate(mults):
        parts = [
            scores[t * rows : (t + 1) * rows, j * span : (j + 1) * span] * SCALE
            + jnp.where(mult > 0, 0.0, MASKED)
            for j, mult in enumerate(counted)
        ]
        top = jnp.max(functools.reduce(jnp.maximum, parts), axis=-1, keepdims=True)
        weights = [jnp.exp2(part - top) * mult for part, mult in zip(parts, counted)]
        totals.append(jnp.sum(functools.reduce(jnp.add, weights), axis=-1, keepdims=True))
        rounded.append(jnp.concatenate([one.astype(jnp.bfloat16) for one in weights], axis=1))
    mixed = jnp.dot(jnp.concatenate(rounded, axis=0), value, preferred_element_type=jnp.float32)
    return mixed / jnp.concatenate(totals, axis=0)


def finish(residual, gate, attention):
    return (residual.astype(jnp.float32) + gate * attention).astype(jnp.bfloat16)


def relay_kernel(first, heads, block, mult_ref, *refs):
    pairs, rests, g_ref, outs = refs[:8], refs[8:12], refs[12], refs[13:]
    rows = pairs[0].shape[0] // 2
    for h in range(block):
        head = first + pl.program_id(0) * block + h
        cols = slice(h * HEAD_DIM, (h + 1) * HEAD_DIM)
        mults = [[mult_ref[(t * heads + head) * 8 + j] for j in range(8)] for t in range(4)]
        mixed = attend(
            jnp.concatenate([ref[:rows, cols] for ref in rests], axis=0),
            jnp.concatenate([ref[:rows, cols] for ref in pairs], axis=0),
            jnp.concatenate([ref[rows:, cols] for ref in pairs], axis=0),
            mults,
        )
        for t, (rest, o_ref) in enumerate(zip(rests, outs)):
            part = mixed[t * rows : (t + 1) * rows]
            o_ref[:, cols] = finish(rest[rows:, cols], g_ref[:, cols], part)


def multiplicity(lists, valid, me, tiles):
    tile = jnp.arange(tiles)
    near = (jnp.abs(tile - me) <= 1).astype(jnp.int32)
    chosen = (lists[:, :, None] == tile[None, None, :]) & (
        jnp.arange(K_LIST)[None, :] < valid[:, None]
    )[:, :, None]
    return (near[None, :] + jnp.sum(chosen.astype(jnp.int32), axis=1)).astype(jnp.float32)


def shifted(block, axis, distance):
    devices = range(lax.axis_size(axis))
    return lax.ppermute(block, axis, [((i - distance) % len(devices), i) for i in devices])


def relay_section(queries, keys, values, residual, gate, tile_lists, counts):
    rows = queries.shape[1]
    tiles = lax.axis_size("ctx")
    sections = lax.axis_size("pipe")
    me = lax.axis_index("ctx")
    chip, core = me // 2, me % 2
    half = HEADS // 2
    width = half * HEAD_DIM

    swap = [(i, i ^ 1) for i in range(8)]
    idle = [(0, 1), (1, 0), (6, 7), (7, 6)]
    inward, inward_x = ([(i, i ^ change) for i in range(8)] for change in (2, 3))
    across, across_x = ([(i, (i ^ 6) ^ change) for i in (2, 3, 4, 5)] + idle for change in (0, 1))

    def onward(change):
        return [
            (p * tiles + i, (p + 1) % sections * tiles + (i ^ change))
            for p in range(sections)
            for i in range(tiles)
        ]

    def ctx(block, route, name):
        with jax.named_scope(name):
            return lax.ppermute(block, "ctx", route)

    def after(block, *others):
        return lax.optimization_barrier((block, *others))[0]

    def halves(block):
        left, right = jnp.split(block, 2, axis=-1)
        return jnp.where(core == 0, left, right), jnp.where(core == 0, right, left)

    edges = [0]
    for size in GROUPS:
        edges.append(edges[-1] + size)
    cut = [slice(a * HEAD_DIM, b * HEAD_DIM) for a, b in zip(edges, edges[1:])]

    def picked(cols):
        pairs = []
        for array in (keys[0], values[0]):
            left, right = array[:, cols], array[:, width + cols.start : width + cols.stop]
            pairs.append((jnp.where(core == 0, left, right), jnp.where(core == 0, right, left)))
        return [jnp.concatenate(pair, axis=0) for pair in zip(*pairs)]

    mine, theirs = picked(cut[0])
    near0, near1 = ctx(mine, across, "near_a0"), ctx(theirs, across_x, "near_a1")
    end0 = ctx(mine, inward, "end_a0")
    sibling = ctx(theirs, swap, "swap_a")
    table = multiplicity(tile_lists[0, 0], counts[0, 0], me, tiles).reshape(2, half, tiles)
    table_mine = jnp.where(core == 0, table[0], table[1])
    table_theirs = jnp.where(core == 0, table[1], table[0])
    tables = [table_mine, ctx(table_theirs, swap, "table_swap")]
    tables += [ctx(table_mine, inward, "table_end0"), ctx(table_theirs, inward_x, "table_end1")]
    end1 = ctx(after(theirs, *tables), inward_x, "end_a1")

    kv_mine, kv_theirs = picked(slice(cut[0].stop, width))
    qr_mine, qr_theirs = halves(jnp.concatenate([queries[0], residual[0]], axis=0))
    got = ctx(after(jnp.concatenate([kv_theirs, qr_theirs], axis=1), sibling), swap, "swap_rest")
    start = cut[0].stop
    own = [
        jnp.concatenate([part[:, c.start - start : c.stop - start] for part in (kv_mine, got)], axis=0)
        for c in cut[1:]
    ]
    qr_got = got[:, width - start :]
    own_qr = [jnp.concatenate([qr_mine[:, c], qr_got[:, c]], axis=0) for c in cut]

    near_b = ctx(own[0], across, "near_b")
    end_b = ctx(after(own[0], end0), inward, "end_b")
    far0, far1 = ctx(end0, across, "far_a0"), ctx(end1, across, "far_a1")
    qr_a = ctx(after(own_qr[0], end1), inward, "qr_a")
    qr_b = ctx(after(own_qr[1], end_b), inward, "qr_b")
    far_b = ctx(end_b, across, "far_b")
    near_c = ctx(after(own[1], end_b), across, "near_c")
    end_c = ctx(after(own[1], qr_a), inward, "end_c")
    far_c = ctx(end_c, across, "far_c")
    qr_c = ctx(after(own_qr[2], qr_b), inward, "qr_c")

    chips = jnp.stack([chip, chip ^ 1, 3 - chip, 3 - (chip ^ 1)])
    order = (2 * chips[:, None] + jnp.stack([core, 1 - core])[None, :]).reshape(1, 1, 8, 1)
    table = jnp.stack(tables)
    table = jnp.sum(jnp.where(order == jnp.arange(tiles), table[:, :, None, :], 0.0), axis=-1)
    table = table.reshape(4 * half * tiles)
    gate_mine, _ = halves(gate)

    def twice(block):
        return [(block, 0), (block, 1)]

    whole = lambda *blocks: [(block, 0) for block in blocks]
    pairs = [
        whole(mine, sibling, end0, end1, near0, near1, far0, far1),
        twice(own[0]) + twice(end_b) + twice(near_b) + twice(far_b),
        twice(own[1]) + twice(end_c) + twice(near_c) + twice(far_c),
    ]
    rests = [twice(own_qr[g]) + twice(block) for g, block in enumerate((qr_a, qr_b, qr_c))]
    same, other = [], []
    inner = (chip == 1) | (chip == 2)
    for g, (size, block) in enumerate(zip(GROUPS, BLOCKS)):
        cols = block * HEAD_DIM
        inputs = pairs[g] + rests[g] + [(gate_mine[:, cut[g]], 0)]
        heights = [2 * rows] * 12 + [1]
        results = pl.pallas_call(
            functools.partial(relay_kernel, edges[g], half, block),
            out_shape=[jax.ShapeDtypeStruct((rows, size * HEAD_DIM), jnp.bfloat16)] * 4,
            grid_spec=pltpu.PrefetchScalarGridSpec(
                num_scalar_prefetch=1,
                grid=(size // block,),
                in_specs=[
                    pl.BlockSpec((height, cols), lambda h, m, place=place: (place, h))
                    for height, (_, place) in zip(heights, inputs)
                ],
                out_specs=[pl.BlockSpec((rows, cols), lambda h, m: (0, h))] * 4,
            ),
            cost_estimate=pl.CostEstimate(
                flops=size * COST * rows * 8 * rows * HEAD_DIM,
                bytes_accessed=size * 28 * rows * HEAD_DIM * 2,
                transcendentals=size * 4 * rows * 8 * rows,
            ),
        )(table, *(array for array, _ in inputs))
        table = after(table, results[0])
        sent = [
            lax.ppermute(piece, ("pipe", "ctx"), onward(change))
            for piece, change in zip(results, (0, 1, 2, 3))
        ]
        same.append(jnp.where(inner, sent[0], sent[2]))
        other.append(jnp.where(inner, sent[1], sent[3]))
    same, other = jnp.concatenate(same, axis=1), jnp.concatenate(other, axis=1)
    left, right = jnp.where(core == 0, same, other), jnp.where(core == 0, other, same)
    return jnp.concatenate([left, right], axis=1)[None]


def pick_kernel(head_ref, k_ref, v_ref, o_ref):
    o_ref[0, :, :HEAD_DIM] = k_ref[...]
    o_ref[0, :, HEAD_DIM:] = v_ref[...]


def listed_kernel(pick_ref, valid_ref, edge_ref, q_ref, *refs):
    near_k, near_v, far = refs[:3], refs[3:6], refs[6 : 6 + K_LIST]
    r_ref, g_ref, o_ref = refs[6 + K_LIST :]
    head = pl.program_id(0)
    one = jnp.float32(1.0)
    mults = [edge_ref[0].astype(jnp.float32), one, edge_ref[1].astype(jnp.float32)]
    mults += [jnp.where(k < valid_ref[head], 1.0, 0.0) for k in range(K_LIST)]
    keys = [ref[...] for ref in near_k] + [ref[0, :, :HEAD_DIM] for ref in far]
    vals = [ref[...] for ref in near_v] + [ref[0, :, HEAD_DIM:] for ref in far]
    mixed = attend(q_ref[...], jnp.concatenate(keys, axis=0), jnp.concatenate(vals, axis=0), [mults])
    o_ref[...] = finish(r_ref[...], g_ref[...], mixed)


def listed_section(queries, keys, values, residual, gate, tile_lists, counts):
    rows = queries.shape[1]
    tiles = lax.axis_size("ctx")
    me = lax.axis_index("ctx")
    cap = (HEADS * K_LIST + tiles - 2) // (tiles - 1)
    lists = tile_lists[0, 0]
    up = [(i, i + 1) for i in range(tiles - 1)]
    down = [(j, i) for i, j in up]
    near_k = [lax.ppermute(keys[0], "ctx", up), keys[0], lax.ppermute(keys[0], "ctx", down)]
    near_v = [lax.ppermute(values[0], "ctx", up), values[0], lax.ppermute(values[0], "ctx", down)]
    flat = lax.all_gather(lists.reshape(1, HEADS * K_LIST), "ctx", axis=0, tiled=True)

    def entry_ranks(entries):
        same = entries[:, None] == entries[None, :]
        earlier = entry[None, :] < entry[:, None]
        return jnp.sum((same & earlier).astype(jnp.int32), axis=-1)

    mine = flat == me
    entry = jnp.arange(HEADS * K_LIST)
    before = (entry[:, None] < entry[None, :]).astype(jnp.float32)
    rank = jnp.dot(mine.astype(jnp.float32), before).astype(jnp.int32)
    head_of = jnp.arange(HEADS * K_LIST) // K_LIST
    slot = jnp.arange(cap)
    hit = mine[:, :, None] & (rank[:, :, None] == slot[None, None, :])
    heads = jnp.sum(jnp.where(hit, head_of[None, :, None], 0), axis=1).reshape(tiles * cap)
    pair = pl.BlockSpec((rows, HEAD_DIM), lambda i, h: (0, h[i]))
    outgoing = pl.pallas_call(
        pick_kernel,
        out_shape=jax.ShapeDtypeStruct((tiles * cap, rows, 2 * HEAD_DIM), jnp.bfloat16),
        grid_spec=pltpu.PrefetchScalarGridSpec(
            num_scalar_prefetch=1,
            grid=(tiles * cap,),
            in_specs=[pair, pair],
            out_specs=pl.BlockSpec((1, rows, 2 * HEAD_DIM), lambda i, h: (i, 0, 0)),
        ),
    )(heads, keys[0], values[0])
    arrived = lax.all_to_all(outgoing, "ctx", split_axis=0, concat_axis=0, tiled=True)
    own_entries = lists.reshape(HEADS * K_LIST)
    pick = own_entries * cap + entry_ranks(own_entries)
    edge = jnp.stack([me > 0, me < tiles - 1]).astype(jnp.int32)
    own = pl.BlockSpec((rows, HEAD_DIM), lambda h, p, c, e: (0, h))
    far = [
        pl.BlockSpec((1, rows, 2 * HEAD_DIM), lambda h, p, c, e, k=k: (p[h * K_LIST + k], 0, 0))
        for k in range(K_LIST)
    ]
    updated = pl.pallas_call(
        listed_kernel,
        out_shape=jax.ShapeDtypeStruct((rows, HEADS * HEAD_DIM), jnp.bfloat16),
        grid_spec=pltpu.PrefetchScalarGridSpec(
            num_scalar_prefetch=3,
            grid=(HEADS,),
            in_specs=[own] * 7 + far + [own, pl.BlockSpec((1, HEAD_DIM), lambda h, p, c, e: (0, h))],
            out_specs=own,
        ),
    )(pick, counts[0, 0], edge, queries[0], *near_k, *near_v, *([arrived] * K_LIST), residual[0], gate)
    return shifted(updated[None], "pipe", 1)


def solution(mesh):
    rows = P("pipe", "ctx", None)
    placed = (rows, rows, rows, rows, P("pipe", None), P("pipe", "ctx", None, None), rows)
    section = relay_section if mesh.shape["ctx"] == 8 else listed_section
    return jax.shard_map(section, mesh=mesh, in_specs=placed, out_specs=rows, check_vma=False)
```

```python
import functools
import math

import jax
import jax.numpy as jnp
from jax import lax
from jax.experimental import pallas as pl
from jax.experimental.pallas import tpu as pltpu
from jax.sharding import PartitionSpec as P

HEADS = 24
HEAD_DIM = 128
K_LIST = 5
GROUPS = (7, 5)
PARTS = ((0, 0, 7, 7), (1, 0, 5, 5))
COST = 96
SCALE = math.log2(math.e) / math.sqrt(HEAD_DIM)
MASKED = -1e30


def dot_nt(a, b):
    return lax.dot_general(a, b, (((1,), (1,)), ((), ())), preferred_element_type=jnp.float32)


def attend(query, key, value, mults):
    scores = dot_nt(query, key)
    rows = query.shape[0] // len(mults)
    span = key.shape[0] // len(mults[0])
    rounded, totals = [], []
    for t, counted in enumerate(mults):
        parts = [
            scores[t * rows : (t + 1) * rows, j * span : (j + 1) * span] * SCALE
            + jnp.where(mult > 0, 0.0, MASKED)
            for j, mult in enumerate(counted)
        ]
        top = jnp.max(functools.reduce(jnp.maximum, parts), axis=-1, keepdims=True)
        weights = [jnp.exp2(part - top) * mult for part, mult in zip(parts, counted)]
        totals.append(jnp.sum(functools.reduce(jnp.add, weights), axis=-1, keepdims=True))
        rounded.append(jnp.concatenate([one.astype(jnp.bfloat16) for one in weights], axis=1))
    mixed = jnp.dot(jnp.concatenate(rounded, axis=0), value, preferred_element_type=jnp.float32)
    return mixed / jnp.concatenate(totals, axis=0)


def finish(residual, gate, attention):
    return (residual.astype(jnp.float32) + gate * attention).astype(jnp.bfloat16)


def relay_kernel(first, heads, block, mult_ref, *refs):
    pairs, rests, g_ref, outs = refs[:8], refs[8:12], refs[12], refs[13:]
    rows = pairs[0].shape[0] // 2
    for h in range(block):
        head = first + pl.program_id(0) * block + h
        cols = slice(h * HEAD_DIM, (h + 1) * HEAD_DIM)
        mults = [[mult_ref[(t * heads + head) * 8 + j] for j in range(8)] for t in range(4)]
        mixed = attend(
            jnp.concatenate([ref[:rows, cols] for ref in rests], axis=0),
            jnp.concatenate([ref[:rows, cols] for ref in pairs], axis=0),
            jnp.concatenate([ref[rows:, cols] for ref in pairs], axis=0),
            mults,
        )
        for t, (rest, o_ref) in enumerate(zip(rests, outs)):
            part = mixed[t * rows : (t + 1) * rows]
            o_ref[:, cols] = finish(rest[rows:, cols], g_ref[:, cols], part)


def multiplicity(lists, valid, me, tiles):
    tile = jnp.arange(tiles)
    near = (jnp.abs(tile - me) <= 1).astype(jnp.int32)
    chosen = (lists[:, :, None] == tile[None, None, :]) & (
        jnp.arange(K_LIST)[None, :] < valid[:, None]
    )[:, :, None]
    return (near[None, :] + jnp.sum(chosen.astype(jnp.int32), axis=1)).astype(jnp.float32)


def shifted(block, axis, distance):
    devices = range(lax.axis_size(axis))
    return lax.ppermute(block, axis, [((i - distance) % len(devices), i) for i in devices])


def relay_section(queries, keys, values, residual, gate, tile_lists, counts):
    rows = queries.shape[1]
    tiles = lax.axis_size("ctx")
    sections = lax.axis_size("pipe")
    me = lax.axis_index("ctx")
    chip, core = me // 2, me % 2
    half = HEADS // 2
    width = half * HEAD_DIM

    swap = [(i, i ^ 1) for i in range(8)]
    idle = [(0, 1), (1, 0), (6, 7), (7, 6)]
    inward, inward_x = ([(i, i ^ change) for i in range(8)] for change in (2, 3))
    across, across_x = ([(i, (i ^ 6) ^ change) for i in (2, 3, 4, 5)] + idle for change in (0, 1))

    def onward(change):
        return [
            (p * tiles + i, (p + 1) % sections * tiles + (i ^ change))
            for p in range(sections)
            for i in range(tiles)
        ]

    def ctx(block, route, name):
        with jax.named_scope(name):
            return lax.ppermute(block, "ctx", route)

    def onto(part, block, route):
        with jax.named_scope(f"onto_{part}"):
            return lax.ppermute(block, ("pipe", "ctx"), route)

    def after(block, *others):
        return lax.optimization_barrier((block, *others))[0]

    def halves(block):
        left, right = jnp.split(block, 2, axis=-1)
        return jnp.where(core == 0, left, right), jnp.where(core == 0, right, left)

    edges = [0]
    for size in GROUPS:
        edges.append(edges[-1] + size)
    cut = [slice(a * HEAD_DIM, b * HEAD_DIM) for a, b in zip(edges, edges[1:])]

    def picked(cols):
        pairs = []
        for array in (keys[0], values[0]):
            left, right = array[:, cols], array[:, width + cols.start : width + cols.stop]
            pairs.append((jnp.where(core == 0, left, right), jnp.where(core == 0, right, left)))
        return [jnp.concatenate(pair, axis=0) for pair in zip(*pairs)]

    mine, theirs = picked(cut[0])
    near0, near1 = ctx(mine, across, "near_a0"), ctx(theirs, across_x, "near_a1")
    end0 = ctx(mine, inward, "end_a0")
    sibling = ctx(theirs, swap, "swap_a")
    table = multiplicity(tile_lists[0, 0], counts[0, 0], me, tiles).reshape(2, half, tiles)
    table_mine = jnp.where(core == 0, table[0], table[1])
    table_theirs = jnp.where(core == 0, table[1], table[0])
    tables = [table_mine, ctx(table_theirs, swap, "table_swap")]
    tables += [ctx(table_mine, inward, "table_end0"), ctx(table_theirs, inward_x, "table_end1")]
    end1 = ctx(after(theirs, *tables), inward_x, "end_a1")

    kv_mine, kv_theirs = picked(slice(cut[0].stop, width))
    qr_mine, qr_theirs = halves(jnp.concatenate([queries[0], residual[0]], axis=0))
    got = ctx(after(jnp.concatenate([kv_theirs, qr_theirs], axis=1), sibling), swap, "swap_rest")
    start = cut[0].stop
    own = [
        jnp.concatenate([part[:, c.start - start : c.stop - start] for part in (kv_mine, got)], axis=0)
        for c in cut[1:]
    ]
    qr_got = got[:, width - start :]
    own_qr = [jnp.concatenate([qr_mine[:, c], qr_got[:, c]], axis=0) for c in cut]

    end_b = ctx(after(own[0], end0), inward, "end_b")
    near_b = ctx(own[0], across, "near_b")
    far0 = ctx(end0, across, "far_a0")
    far1 = ctx(end1, across, "far_a1")
    qr_a = ctx(after(own_qr[0], end1), inward, "qr_a")
    qr_b = ctx(after(own_qr[1], end_b), inward, "qr_b")
    far_b = ctx(end_b, across, "far_b")

    chips = jnp.stack([chip, chip ^ 1, 3 - chip, 3 - (chip ^ 1)])
    order = (2 * chips[:, None] + jnp.stack([core, 1 - core])[None, :]).reshape(1, 1, 8, 1)
    table = jnp.stack(tables)
    table = jnp.sum(jnp.where(order == jnp.arange(tiles), table[:, :, None, :], 0.0), axis=-1)
    table = table.reshape(4 * half * tiles)
    gate_mine, _ = halves(gate)

    def twice(block):
        return [(block, 0), (block, 1)]

    whole = lambda *blocks: [(block, 0) for block in blocks]
    pairs = [
        whole(mine, sibling, end0, end1, near0, near1, far0, far1),
        twice(own[0]) + twice(end_b) + twice(near_b) + twice(far_b),
    ]
    rests = [twice(own_qr[g]) + twice(block) for g, block in enumerate((qr_a, qr_b))]
    same, other = [], []
    inner = (chip == 1) | (chip == 2)
    for part, (g, start, size, block) in enumerate(PARTS):
        cols = block * HEAD_DIM
        first = edges[g] + start
        skip = start // block
        inputs = pairs[g] + rests[g]
        inputs = [(array, place, skip) for array, place in inputs]
        inputs += [(gate_mine[:, first * HEAD_DIM : (first + size) * HEAD_DIM], 0, 0)]
        heights = [2 * rows] * 12 + [1]
        if part == 0:
            table = table
        results = pl.pallas_call(
            functools.partial(relay_kernel, first, half, block),
            out_shape=[jax.ShapeDtypeStruct((rows, size * HEAD_DIM), jnp.bfloat16)] * 4,
            grid_spec=pltpu.PrefetchScalarGridSpec(
                num_scalar_prefetch=1,
                grid=(size // block,),
                in_specs=[
                    pl.BlockSpec((height, cols), lambda h, m, place=place, skip=skip: (place, skip + h))
                    for height, (_, place, skip) in zip(heights, inputs)
                ],
                out_specs=[pl.BlockSpec((rows, cols), lambda h, m: (0, h))] * 4,
            ),
            cost_estimate=pl.CostEstimate(
                flops=size * COST * rows * 8 * rows * HEAD_DIM,
                bytes_accessed=size * 28 * rows * HEAD_DIM * 2,
                transcendentals=size * 4 * rows * 8 * rows,
            ),
        )(table, *(array for array, *_ in inputs))
        table = after(table, results[0])
        sent = [
            onto(part, piece, onward(change))
            for piece, change in zip(results, (0, 1, 2, 3))
        ]
        same.append(jnp.where(inner, sent[0], sent[2]))
        other.append(jnp.where(inner, sent[1], sent[3]))
    same, other = jnp.concatenate(same, axis=1), jnp.concatenate(other, axis=1)
    left, right = jnp.where(core == 0, same, other), jnp.where(core == 0, other, same)
    return jnp.concatenate([left, right], axis=1)[None]


def pick_kernel(head_ref, k_ref, v_ref, o_ref):
    o_ref[0, :, :HEAD_DIM] = k_ref[...]
    o_ref[0, :, HEAD_DIM:] = v_ref[...]


def listed_kernel(pick_ref, valid_ref, edge_ref, q_ref, *refs):
    near_k, near_v, far = refs[:3], refs[3:6], refs[6 : 6 + K_LIST]
    r_ref, g_ref, o_ref = refs[6 + K_LIST :]
    head = pl.program_id(0)
    one = jnp.float32(1.0)
    mults = [edge_ref[0].astype(jnp.float32), one, edge_ref[1].astype(jnp.float32)]
    mults += [jnp.where(k < valid_ref[head], 1.0, 0.0) for k in range(K_LIST)]
    keys = [ref[...] for ref in near_k] + [ref[0, :, :HEAD_DIM] for ref in far]
    vals = [ref[...] for ref in near_v] + [ref[0, :, HEAD_DIM:] for ref in far]
    mixed = attend(q_ref[...], jnp.concatenate(keys, axis=0), jnp.concatenate(vals, axis=0), [mults])
    o_ref[...] = finish(r_ref[...], g_ref[...], mixed)


def listed_section(queries, keys, values, residual, gate, tile_lists, counts):
    rows = queries.shape[1]
    tiles = lax.axis_size("ctx")
    me = lax.axis_index("ctx")
    cap = (HEADS * K_LIST + tiles - 2) // (tiles - 1)
    lists = tile_lists[0, 0]
    up = [(i, i + 1) for i in range(tiles - 1)]
    down = [(j, i) for i, j in up]
    near_k = [lax.ppermute(keys[0], "ctx", up), keys[0], lax.ppermute(keys[0], "ctx", down)]
    near_v = [lax.ppermute(values[0], "ctx", up), values[0], lax.ppermute(values[0], "ctx", down)]
    flat = lax.all_gather(lists.reshape(1, HEADS * K_LIST), "ctx", axis=0, tiled=True)

    def entry_ranks(entries):
        same = entries[:, None] == entries[None, :]
        earlier = entry[None, :] < entry[:, None]
        return jnp.sum((same & earlier).astype(jnp.int32), axis=-1)

    mine = flat == me
    entry = jnp.arange(HEADS * K_LIST)
    before = (entry[:, None] < entry[None, :]).astype(jnp.float32)
    rank = jnp.dot(mine.astype(jnp.float32), before).astype(jnp.int32)
    head_of = jnp.arange(HEADS * K_LIST) // K_LIST
    slot = jnp.arange(cap)
    hit = mine[:, :, None] & (rank[:, :, None] == slot[None, None, :])
    heads = jnp.sum(jnp.where(hit, head_of[None, :, None], 0), axis=1).reshape(tiles * cap)
    pair = pl.BlockSpec((rows, HEAD_DIM), lambda i, h: (0, h[i]))
    outgoing = pl.pallas_call(
        pick_kernel,
        out_shape=jax.ShapeDtypeStruct((tiles * cap, rows, 2 * HEAD_DIM), jnp.bfloat16),
        grid_spec=pltpu.PrefetchScalarGridSpec(
            num_scalar_prefetch=1,
            grid=(tiles * cap,),
            in_specs=[pair, pair],
            out_specs=pl.BlockSpec((1, rows, 2 * HEAD_DIM), lambda i, h: (i, 0, 0)),
        ),
    )(heads, keys[0], values[0])
    arrived = lax.all_to_all(outgoing, "ctx", split_axis=0, concat_axis=0, tiled=True)
    own_entries = lists.reshape(HEADS * K_LIST)
    pick = own_entries * cap + entry_ranks(own_entries)
    edge = jnp.stack([me > 0, me < tiles - 1]).astype(jnp.int32)
    own = pl.BlockSpec((rows, HEAD_DIM), lambda h, p, c, e: (0, h))
    far = [
        pl.BlockSpec((1, rows, 2 * HEAD_DIM), lambda h, p, c, e, k=k: (p[h * K_LIST + k], 0, 0))
        for k in range(K_LIST)
    ]
    updated = pl.pallas_call(
        listed_kernel,
        out_shape=jax.ShapeDtypeStruct((rows, HEADS * HEAD_DIM), jnp.bfloat16),
        grid_spec=pltpu.PrefetchScalarGridSpec(
            num_scalar_prefetch=3,
            grid=(HEADS,),
            in_specs=[own] * 7 + far + [own, pl.BlockSpec((1, HEAD_DIM), lambda h, p, c, e: (0, h))],
            out_specs=own,
        ),
    )(pick, counts[0, 0], edge, queries[0], *near_k, *near_v, *([arrived] * K_LIST), residual[0], gate)
    return shifted(updated[None], "pipe", 1)


def solution(mesh):
    rows = P("pipe", "ctx", None)
    placed = (rows, rows, rows, rows, P("pipe", None), P("pipe", "ctx", None, None), rows)
    section = relay_section if mesh.shape["ctx"] == 8 else listed_section
    return jax.shard_map(section, mesh=mesh, in_specs=placed, out_specs=rows, check_vma=False)
```

```python
import functools
import math

import jax
import jax.numpy as jnp
from jax import lax
from jax.experimental import pallas as pl
from jax.experimental.pallas import tpu as pltpu
from jax.sharding import PartitionSpec as P

HEADS = 24
HEAD_DIM = 128
K_LIST = 5
GROUPS = (7, 5)
PARTS = ((0, 0, 7, 7), (1, 0, 5, 5))
COST = 96
SCALE = math.log2(math.e) / math.sqrt(HEAD_DIM)
MASKED = -1e30


def dot_nt(a, b):
    return lax.dot_general(a, b, (((1,), (1,)), ((), ())), preferred_element_type=jnp.float32)


def attend(query, key, value, mults):
    scores = dot_nt(query, key)
    rows = query.shape[0] // len(mults)
    span = key.shape[0] // len(mults[0])
    rounded, totals = [], []
    for t, counted in enumerate(mults):
        parts = [
            scores[t * rows : (t + 1) * rows, j * span : (j + 1) * span] * SCALE
            + jnp.where(mult > 0, 0.0, MASKED)
            for j, mult in enumerate(counted)
        ]
        top = jnp.max(functools.reduce(jnp.maximum, parts), axis=-1, keepdims=True)
        weights = [jnp.exp2(part - top) * mult for part, mult in zip(parts, counted)]
        totals.append(jnp.sum(functools.reduce(jnp.add, weights), axis=-1, keepdims=True))
        rounded.append(jnp.concatenate([one.astype(jnp.bfloat16) for one in weights], axis=1))
    mixed = jnp.dot(jnp.concatenate(rounded, axis=0), value, preferred_element_type=jnp.float32)
    return mixed / jnp.concatenate(totals, axis=0)


def finish(residual, gate, attention):
    return (residual.astype(jnp.float32) + gate * attention).astype(jnp.bfloat16)


def relay_kernel(first, heads, block, mult_ref, *refs):
    pairs, rests, g_ref, outs = refs[:8], refs[8:12], refs[12], refs[13:]
    rows = pairs[0].shape[0] // 2
    for h in range(block):
        head = first + pl.program_id(0) * block + h
        cols = slice(h * HEAD_DIM, (h + 1) * HEAD_DIM)
        mults = [[mult_ref[(t * heads + head) * 8 + j] for j in range(8)] for t in range(4)]
        mixed = attend(
            jnp.concatenate([ref[:rows, cols] for ref in rests], axis=0),
            jnp.concatenate([ref[:rows, cols] for ref in pairs], axis=0),
            jnp.concatenate([ref[rows:, cols] for ref in pairs], axis=0),
            mults,
        )
        for t, rest in enumerate(rests):
            part = mixed[t * rows : (t + 1) * rows]
            place = slice(t % 2 * rows, (t % 2 + 1) * rows)
            outs[t // 2][place, cols] = finish(rest[rows:, cols], g_ref[:, cols], part)


def multiplicity(lists, valid, me, tiles):
    tile = jnp.arange(tiles)
    near = (jnp.abs(tile - me) <= 1).astype(jnp.int32)
    chosen = (lists[:, :, None] == tile[None, None, :]) & (
        jnp.arange(K_LIST)[None, :] < valid[:, None]
    )[:, :, None]
    return (near[None, :] + jnp.sum(chosen.astype(jnp.int32), axis=1)).astype(jnp.float32)


def shifted(block, axis, distance):
    devices = range(lax.axis_size(axis))
    return lax.ppermute(block, axis, [((i - distance) % len(devices), i) for i in devices])


def relay_section(queries, keys, values, residual, gate, tile_lists, counts):
    rows = queries.shape[1]
    tiles = lax.axis_size("ctx")
    sections = lax.axis_size("pipe")
    me = lax.axis_index("ctx")
    chip, core = me // 2, me % 2
    half = HEADS // 2
    width = half * HEAD_DIM

    swap = [(i, i ^ 1) for i in range(8)]
    idle = [(0, 1), (1, 0), (6, 7), (7, 6)]
    inward, inward_x = ([(i, i ^ change) for i in range(8)] for change in (2, 3))
    across, across_x = ([(i, (i ^ 6) ^ change) for i in (2, 3, 4, 5)] + idle for change in (0, 1))

    def onward(change):
        return [
            (p * tiles + i, (p + 1) % sections * tiles + (i ^ change))
            for p in range(sections)
            for i in range(tiles)
        ]

    def ctx(block, route, name):
        with jax.named_scope(name):
            return lax.ppermute(block, "ctx", route)

    def onto(part, block, route):
        with jax.named_scope(f"onto_{part}"):
            return lax.ppermute(block, ("pipe", "ctx"), route)

    def after(block, *others):
        return lax.optimization_barrier((block, *others))[0]

    def halves(block):
        left, right = jnp.split(block, 2, axis=-1)
        return jnp.where(core == 0, left, right), jnp.where(core == 0, right, left)

    edges = [0]
    for size in GROUPS:
        edges.append(edges[-1] + size)
    cut = [slice(a * HEAD_DIM, b * HEAD_DIM) for a, b in zip(edges, edges[1:])]

    def picked(cols):
        pairs = []
        for array in (keys[0], values[0]):
            left, right = array[:, cols], array[:, width + cols.start : width + cols.stop]
            pairs.append((jnp.where(core == 0, left, right), jnp.where(core == 0, right, left)))
        return [jnp.concatenate(pair, axis=0) for pair in zip(*pairs)]

    mine, theirs = picked(cut[0])
    near0, near1 = ctx(mine, across, "near_a0"), ctx(theirs, across_x, "near_a1")
    end0 = ctx(mine, inward, "end_a0")
    sibling = ctx(theirs, swap, "swap_a")
    table = multiplicity(tile_lists[0, 0], counts[0, 0], me, tiles).reshape(2, half, tiles)
    table_mine = jnp.where(core == 0, table[0], table[1])
    table_theirs = jnp.where(core == 0, table[1], table[0])
    tables = [table_mine, ctx(table_theirs, swap, "table_swap")]
    tables += [ctx(table_mine, inward, "table_end0"), ctx(table_theirs, inward_x, "table_end1")]
    end1 = ctx(after(theirs, *tables), inward_x, "end_a1")

    kv_mine, kv_theirs = picked(slice(cut[0].stop, width))
    qr_mine, qr_theirs = halves(jnp.concatenate([queries[0], residual[0]], axis=0))
    got = ctx(after(jnp.concatenate([kv_theirs, qr_theirs], axis=1), sibling), swap, "swap_rest")
    start = cut[0].stop
    own = [
        jnp.concatenate([part[:, c.start - start : c.stop - start] for part in (kv_mine, got)], axis=0)
        for c in cut[1:]
    ]
    qr_got = got[:, width - start :]
    own_qr = [jnp.concatenate([qr_mine[:, c], qr_got[:, c]], axis=0) for c in cut]

    end_b = ctx(after(own[0], end0), inward, "end_b")
    near_b = ctx(own[0], across, "near_b")
    far0 = ctx(end0, across, "far_a0")
    far1 = ctx(end1, across, "far_a1")
    qr_a = ctx(after(own_qr[0], end1), inward, "qr_a")
    qr_b = ctx(after(own_qr[1], end_b), inward, "qr_b")
    far_b = ctx(end_b, across, "far_b")

    chips = jnp.stack([chip, chip ^ 1, 3 - chip, 3 - (chip ^ 1)])
    order = (2 * chips[:, None] + jnp.stack([core, 1 - core])[None, :]).reshape(1, 1, 8, 1)
    table = jnp.stack(tables)
    table = jnp.sum(jnp.where(order == jnp.arange(tiles), table[:, :, None, :], 0.0), axis=-1)
    table = table.reshape(4 * half * tiles)
    gate_mine, _ = halves(gate)

    def twice(block):
        return [(block, 0), (block, 1)]

    whole = lambda *blocks: [(block, 0) for block in blocks]
    pairs = [
        whole(mine, sibling, end0, end1, near0, near1, far0, far1),
        twice(own[0]) + twice(end_b) + twice(near_b) + twice(far_b),
    ]
    rests = [twice(own_qr[g]) + twice(block) for g, block in enumerate((qr_a, qr_b))]
    same, other = [], []
    inner = (chip == 1) | (chip == 2)
    for part, (g, start, size, block) in enumerate(PARTS):
        cols = block * HEAD_DIM
        first = edges[g] + start
        skip = start // block
        inputs = pairs[g] + rests[g]
        inputs = [(array, place, skip) for array, place in inputs]
        inputs += [(gate_mine[:, first * HEAD_DIM : (first + size) * HEAD_DIM], 0, 0)]
        heights = [2 * rows] * 12 + [1]
        if part == 0:
            table = table
        results = pl.pallas_call(
            functools.partial(relay_kernel, first, half, block),
            out_shape=[jax.ShapeDtypeStruct((2 * rows, size * HEAD_DIM), jnp.bfloat16)] * 2,
            grid_spec=pltpu.PrefetchScalarGridSpec(
                num_scalar_prefetch=1,
                grid=(size // block,),
                in_specs=[
                    pl.BlockSpec((height, cols), lambda h, m, place=place, skip=skip: (place, skip + h))
                    for height, (_, place, skip) in zip(heights, inputs)
                ],
                out_specs=[pl.BlockSpec((2 * rows, cols), lambda h, m: (0, h))] * 2,
            ),
            cost_estimate=pl.CostEstimate(
                flops=size * COST * rows * 8 * rows * HEAD_DIM,
                bytes_accessed=size * 28 * rows * HEAD_DIM * 2,
                transcendentals=size * 4 * rows * 8 * rows,
            ),
        )(table, *(array for array, *_ in inputs))
        table = after(table, results[0])
        sent = [onto(part, piece, onward(change)) for piece, change in zip(results, (0, 2))]
        here = jnp.where(inner, *sent)
        same.append(here[:rows])
        other.append(ctx(here[rows:], swap, f"settle_{part}"))
    same, other = jnp.concatenate(same, axis=1), jnp.concatenate(other, axis=1)
    left, right = jnp.where(core == 0, same, other), jnp.where(core == 0, other, same)
    return jnp.concatenate([left, right], axis=1)[None]


def pick_kernel(head_ref, k_ref, v_ref, o_ref):
    o_ref[0, :, :HEAD_DIM] = k_ref[...]
    o_ref[0, :, HEAD_DIM:] = v_ref[...]


def listed_kernel(pick_ref, valid_ref, edge_ref, q_ref, *refs):
    near_k, near_v, far = refs[:3], refs[3:6], refs[6 : 6 + K_LIST]
    r_ref, g_ref, o_ref = refs[6 + K_LIST :]
    head = pl.program_id(0)
    one = jnp.float32(1.0)
    mults = [edge_ref[0].astype(jnp.float32), one, edge_ref[1].astype(jnp.float32)]
    mults += [jnp.where(k < valid_ref[head], 1.0, 0.0) for k in range(K_LIST)]
    keys = [ref[...] for ref in near_k] + [ref[0, :, :HEAD_DIM] for ref in far]
    vals = [ref[...] for ref in near_v] + [ref[0, :, HEAD_DIM:] for ref in far]
    mixed = attend(q_ref[...], jnp.concatenate(keys, axis=0), jnp.concatenate(vals, axis=0), [mults])
    o_ref[...] = finish(r_ref[...], g_ref[...], mixed)


def listed_section(queries, keys, values, residual, gate, tile_lists, counts):
    rows = queries.shape[1]
    tiles = lax.axis_size("ctx")
    me = lax.axis_index("ctx")
    cap = (HEADS * K_LIST + tiles - 2) // (tiles - 1)
    lists = tile_lists[0, 0]
    up = [(i, i + 1) for i in range(tiles - 1)]
    down = [(j, i) for i, j in up]
    near_k = [lax.ppermute(keys[0], "ctx", up), keys[0], lax.ppermute(keys[0], "ctx", down)]
    near_v = [lax.ppermute(values[0], "ctx", up), values[0], lax.ppermute(values[0], "ctx", down)]
    flat = lax.all_gather(lists.reshape(1, HEADS * K_LIST), "ctx", axis=0, tiled=True)

    def entry_ranks(entries):
        same = entries[:, None] == entries[None, :]
        earlier = entry[None, :] < entry[:, None]
        return jnp.sum((same & earlier).astype(jnp.int32), axis=-1)

    mine = flat == me
    entry = jnp.arange(HEADS * K_LIST)
    before = (entry[:, None] < entry[None, :]).astype(jnp.float32)
    rank = jnp.dot(mine.astype(jnp.float32), before).astype(jnp.int32)
    head_of = jnp.arange(HEADS * K_LIST) // K_LIST
    slot = jnp.arange(cap)
    hit = mine[:, :, None] & (rank[:, :, None] == slot[None, None, :])
    heads = jnp.sum(jnp.where(hit, head_of[None, :, None], 0), axis=1).reshape(tiles * cap)
    pair = pl.BlockSpec((rows, HEAD_DIM), lambda i, h: (0, h[i]))
    outgoing = pl.pallas_call(
        pick_kernel,
        out_shape=jax.ShapeDtypeStruct((tiles * cap, rows, 2 * HEAD_DIM), jnp.bfloat16),
        grid_spec=pltpu.PrefetchScalarGridSpec(
            num_scalar_prefetch=1,
            grid=(tiles * cap,),
            in_specs=[pair, pair],
            out_specs=pl.BlockSpec((1, rows, 2 * HEAD_DIM), lambda i, h: (i, 0, 0)),
        ),
    )(heads, keys[0], values[0])
    arrived = lax.all_to_all(outgoing, "ctx", split_axis=0, concat_axis=0, tiled=True)
    own_entries = lists.reshape(HEADS * K_LIST)
    pick = own_entries * cap + entry_ranks(own_entries)
    edge = jnp.stack([me > 0, me < tiles - 1]).astype(jnp.int32)
    own = pl.BlockSpec((rows, HEAD_DIM), lambda h, p, c, e: (0, h))
    far = [
        pl.BlockSpec((1, rows, 2 * HEAD_DIM), lambda h, p, c, e, k=k: (p[h * K_LIST + k], 0, 0))
        for k in range(K_LIST)
    ]
    updated = pl.pallas_call(
        listed_kernel,
        out_shape=jax.ShapeDtypeStruct((rows, HEADS * HEAD_DIM), jnp.bfloat16),
        grid_spec=pltpu.PrefetchScalarGridSpec(
            num_scalar_prefetch=3,
            grid=(HEADS,),
            in_specs=[own] * 7 + far + [own, pl.BlockSpec((1, HEAD_DIM), lambda h, p, c, e: (0, h))],
            out_specs=own,
        ),
    )(pick, counts[0, 0], edge, queries[0], *near_k, *near_v, *([arrived] * K_LIST), residual[0], gate)
    return shifted(updated[None], "pipe", 1)


def solution(mesh):
    rows = P("pipe", "ctx", None)
    placed = (rows, rows, rows, rows, P("pipe", None), P("pipe", "ctx", None, None), rows)
    section = relay_section if mesh.shape["ctx"] == 8 else listed_section
    return jax.shard_map(section, mesh=mesh, in_specs=placed, out_specs=rows, check_vma=False)
```

```python
import functools
import math

import jax
import jax.numpy as jnp
from jax import lax
from jax.experimental import pallas as pl
from jax.experimental.pallas import tpu as pltpu
from jax.sharding import PartitionSpec as P

HEADS = 24
HEAD_DIM = 128
K_LIST = 5
GROUPS = (7, 5)
PARTS = ((0, 0, 7, 7), (1, 0, 5, 5))
COST = 96
SCALE = math.log2(math.e) / math.sqrt(HEAD_DIM)
MASKED = -1e30


def dot_nt(a, b):
    return lax.dot_general(a, b, (((1,), (1,)), ((), ())), preferred_element_type=jnp.float32)


def attend(query, key, value, mults):
    scores = dot_nt(query, key)
    rows = query.shape[0] // len(mults)
    span = key.shape[0] // len(mults[0])
    rounded, totals = [], []
    for t, counted in enumerate(mults):
        parts = [
            scores[t * rows : (t + 1) * rows, j * span : (j + 1) * span] * SCALE
            + jnp.where(mult > 0, 0.0, MASKED)
            for j, mult in enumerate(counted)
        ]
        top = jnp.max(functools.reduce(jnp.maximum, parts), axis=-1, keepdims=True)
        weights = [jnp.exp2(part - top) * mult for part, mult in zip(parts, counted)]
        totals.append(jnp.sum(functools.reduce(jnp.add, weights), axis=-1, keepdims=True))
        rounded.append(jnp.concatenate([one.astype(jnp.bfloat16) for one in weights], axis=1))
    mixed = jnp.dot(jnp.concatenate(rounded, axis=0), value, preferred_element_type=jnp.float32)
    return mixed / jnp.concatenate(totals, axis=0)


def finish(residual, gate, attention):
    return (residual.astype(jnp.float32) + gate * attention).astype(jnp.bfloat16)


def relay_kernel(first, heads, block, mult_ref, *refs):
    pairs, rests, g_ref, outs = refs[:8], refs[8:12], refs[12], refs[13:]
    rows = pairs[0].shape[0] // 2
    for h in range(block):
        head = first + pl.program_id(0) * block + h
        cols = slice(h * HEAD_DIM, (h + 1) * HEAD_DIM)
        mults = [[mult_ref[(t * heads + head) * 8 + j] for j in range(8)] for t in range(4)]
        mixed = attend(
            jnp.concatenate([ref[:rows, cols] for ref in rests], axis=0),
            jnp.concatenate([ref[:rows, cols] for ref in pairs], axis=0),
            jnp.concatenate([ref[rows:, cols] for ref in pairs], axis=0),
            mults,
        )
        for t, rest in enumerate(rests):
            part = mixed[t * rows : (t + 1) * rows]
            place = slice(t % 2 * rows, (t % 2 + 1) * rows)
            outs[t // 2][place, cols] = finish(rest[rows:, cols], g_ref[:, cols], part)


def multiplicity(lists, valid, me, tiles):
    tile = jnp.arange(tiles)
    near = (jnp.abs(tile - me) <= 1).astype(jnp.int32)
    chosen = (lists[:, :, None] == tile[None, None, :]) & (
        jnp.arange(K_LIST)[None, :] < valid[:, None]
    )[:, :, None]
    return (near[None, :] + jnp.sum(chosen.astype(jnp.int32), axis=1)).astype(jnp.float32)


def shifted(block, axis, distance):
    devices = range(lax.axis_size(axis))
    return lax.ppermute(block, axis, [((i - distance) % len(devices), i) for i in devices])


def relay_section(queries, keys, values, residual, gate, tile_lists, counts):
    rows = queries.shape[1]
    tiles = lax.axis_size("ctx")
    sections = lax.axis_size("pipe")
    me = lax.axis_index("ctx")
    chip, core = me // 2, me % 2
    half = HEADS // 2
    width = half * HEAD_DIM

    swap = [(i, i ^ 1) for i in range(8)]
    idle = [(0, 1), (1, 0), (6, 7), (7, 6)]
    inward, inward_x = ([(i, i ^ change) for i in range(8)] for change in (2, 3))
    across, across_x = ([(i, (i ^ 6) ^ change) for i in (2, 3, 4, 5)] + idle for change in (0, 1))

    outward = [(i, i ^ 2) for i in (2, 3, 4, 5)]

    def onward(change, chips=(0, 1, 2, 3)):
        return [
            (p * tiles + i, (p + 1) % sections * tiles + (i ^ change))
            for p in range(sections)
            for i in range(tiles)
            if i // 2 in chips
        ]

    def ctx(block, route, name):
        with jax.named_scope(name):
            return lax.ppermute(block, "ctx", route)

    def onto(part, block, route):
        with jax.named_scope(f"onto_{part}"):
            return lax.ppermute(block, ("pipe", "ctx"), route)

    def after(block, *others):
        return lax.optimization_barrier((block, *others))[0]

    def halves(block):
        left, right = jnp.split(block, 2, axis=-1)
        return jnp.where(core == 0, left, right), jnp.where(core == 0, right, left)

    edges = [0]
    for size in GROUPS:
        edges.append(edges[-1] + size)
    cut = [slice(a * HEAD_DIM, b * HEAD_DIM) for a, b in zip(edges, edges[1:])]

    def picked(cols):
        pairs = []
        for array in (keys[0], values[0]):
            left, right = array[:, cols], array[:, width + cols.start : width + cols.stop]
            pairs.append((jnp.where(core == 0, left, right), jnp.where(core == 0, right, left)))
        return [jnp.concatenate(pair, axis=0) for pair in zip(*pairs)]

    mine, theirs = picked(cut[0])
    near0, near1 = ctx(mine, across, "near_a0"), ctx(theirs, across_x, "near_a1")
    end0 = ctx(mine, inward, "end_a0")
    sibling = ctx(theirs, swap, "swap_a")
    table = multiplicity(tile_lists[0, 0], counts[0, 0], me, tiles).reshape(2, half, tiles)
    table_mine = jnp.where(core == 0, table[0], table[1])
    table_theirs = jnp.where(core == 0, table[1], table[0])
    tables = [table_mine, ctx(table_theirs, swap, "table_swap")]
    tables += [ctx(table_mine, inward, "table_end0"), ctx(table_theirs, inward_x, "table_end1")]
    end1 = ctx(after(theirs, *tables), inward_x, "end_a1")

    kv_mine, kv_theirs = picked(slice(cut[0].stop, width))
    qr_mine, qr_theirs = halves(jnp.concatenate([queries[0], residual[0]], axis=0))
    got = ctx(after(jnp.concatenate([kv_theirs, qr_theirs], axis=1), sibling), swap, "swap_rest")
    start = cut[0].stop
    own = [
        jnp.concatenate([part[:, c.start - start : c.stop - start] for part in (kv_mine, got)], axis=0)
        for c in cut[1:]
    ]
    qr_got = got[:, width - start :]
    own_qr = [jnp.concatenate([qr_mine[:, c], qr_got[:, c]], axis=0) for c in cut]

    end_b = ctx(after(own[0], end0), inward, "end_b")
    near_b = ctx(own[0], across, "near_b")
    far0 = ctx(end0, across, "far_a0")
    far1 = ctx(end1, across, "far_a1")
    qr_a = ctx(after(own_qr[0], end1), inward, "qr_a")
    qr_b = ctx(after(own_qr[1], end_b), inward, "qr_b")
    far_b = ctx(end_b, across, "far_b")

    chips = jnp.stack([chip, chip ^ 1, 3 - chip, 3 - (chip ^ 1)])
    order = (2 * chips[:, None] + jnp.stack([core, 1 - core])[None, :]).reshape(1, 1, 8, 1)
    table = jnp.stack(tables)
    table = jnp.sum(jnp.where(order == jnp.arange(tiles), table[:, :, None, :], 0.0), axis=-1)
    table = table.reshape(4 * half * tiles)
    gate_mine, _ = halves(gate)

    def twice(block):
        return [(block, 0), (block, 1)]

    whole = lambda *blocks: [(block, 0) for block in blocks]
    pairs = [
        whole(mine, sibling, end0, end1, near0, near1, far0, far1),
        twice(own[0]) + twice(end_b) + twice(near_b) + twice(far_b),
    ]
    rests = [twice(own_qr[g]) + twice(block) for g, block in enumerate((qr_a, qr_b))]
    same, other = [], []
    inner = (chip == 1) | (chip == 2)
    for part, (g, start, size, block) in enumerate(PARTS):
        cols = block * HEAD_DIM
        first = edges[g] + start
        skip = start // block
        inputs = pairs[g] + rests[g]
        inputs = [(array, place, skip) for array, place in inputs]
        inputs += [(gate_mine[:, first * HEAD_DIM : (first + size) * HEAD_DIM], 0, 0)]
        heights = [2 * rows] * 12 + [1]
        if part == 0:
            table = table
        results = pl.pallas_call(
            functools.partial(relay_kernel, first, half, block),
            out_shape=[jax.ShapeDtypeStruct((2 * rows, size * HEAD_DIM), jnp.bfloat16)] * 2,
            grid_spec=pltpu.PrefetchScalarGridSpec(
                num_scalar_prefetch=1,
                grid=(size // block,),
                in_specs=[
                    pl.BlockSpec((height, cols), lambda h, m, place=place, skip=skip: (place, skip + h))
                    for height, (_, place, skip) in zip(heights, inputs)
                ],
                out_specs=[pl.BlockSpec((2 * rows, cols), lambda h, m: (0, h))] * 2,
            ),
            cost_estimate=pl.CostEstimate(
                flops=size * COST * rows * 8 * rows * HEAD_DIM,
                bytes_accessed=size * 28 * rows * HEAD_DIM * 2,
                transcendentals=size * 4 * rows * 8 * rows,
            ),
        )(table, *(array for array, *_ in inputs))
        table = after(table, results[0])
        if part == 0:
            sent = [onto(part, piece, onward(change)) for piece, change in zip(results, (0, 2))]
        else:
            back = ctx(results[1], outward, "back")
            sent = [onto(part, results[0], onward(0, (1, 2))), onto(part, back, onward(0, (0, 3)))]
        here = jnp.where(inner, *sent)
        same.append(here[:rows])
        other.append(ctx(here[rows:], swap, f"settle_{part}"))
    same, other = jnp.concatenate(same, axis=1), jnp.concatenate(other, axis=1)
    left, right = jnp.where(core == 0, same, other), jnp.where(core == 0, other, same)
    return jnp.concatenate([left, right], axis=1)[None]


def pick_kernel(head_ref, k_ref, v_ref, o_ref):
    o_ref[0, :, :HEAD_DIM] = k_ref[...]
    o_ref[0, :, HEAD_DIM:] = v_ref[...]


def listed_kernel(pick_ref, valid_ref, edge_ref, q_ref, *refs):
    near_k, near_v, far = refs[:3], refs[3:6], refs[6 : 6 + K_LIST]
    r_ref, g_ref, o_ref = refs[6 + K_LIST :]
    head = pl.program_id(0)
    one = jnp.float32(1.0)
    mults = [edge_ref[0].astype(jnp.float32), one, edge_ref[1].astype(jnp.float32)]
    mults += [jnp.where(k < valid_ref[head], 1.0, 0.0) for k in range(K_LIST)]
    keys = [ref[...] for ref in near_k] + [ref[0, :, :HEAD_DIM] for ref in far]
    vals = [ref[...] for ref in near_v] + [ref[0, :, HEAD_DIM:] for ref in far]
    mixed = attend(q_ref[...], jnp.concatenate(keys, axis=0), jnp.concatenate(vals, axis=0), [mults])
    o_ref[...] = finish(r_ref[...], g_ref[...], mixed)


def listed_section(queries, keys, values, residual, gate, tile_lists, counts):
    rows = queries.shape[1]
    tiles = lax.axis_size("ctx")
    me = lax.axis_index("ctx")
    cap = (HEADS * K_LIST + tiles - 2) // (tiles - 1)
    lists = tile_lists[0, 0]
    up = [(i, i + 1) for i in range(tiles - 1)]
    down = [(j, i) for i, j in up]
    near_k = [lax.ppermute(keys[0], "ctx", up), keys[0], lax.ppermute(keys[0], "ctx", down)]
    near_v = [lax.ppermute(values[0], "ctx", up), values[0], lax.ppermute(values[0], "ctx", down)]
    flat = lax.all_gather(lists.reshape(1, HEADS * K_LIST), "ctx", axis=0, tiled=True)

    def entry_ranks(entries):
        same = entries[:, None] == entries[None, :]
        earlier = entry[None, :] < entry[:, None]
        return jnp.sum((same & earlier).astype(jnp.int32), axis=-1)

    mine = flat == me
    entry = jnp.arange(HEADS * K_LIST)
    before = (entry[:, None] < entry[None, :]).astype(jnp.float32)
    rank = jnp.dot(mine.astype(jnp.float32), before).astype(jnp.int32)
    head_of = jnp.arange(HEADS * K_LIST) // K_LIST
    slot = jnp.arange(cap)
    hit = mine[:, :, None] & (rank[:, :, None] == slot[None, None, :])
    heads = jnp.sum(jnp.where(hit, head_of[None, :, None], 0), axis=1).reshape(tiles * cap)
    pair = pl.BlockSpec((rows, HEAD_DIM), lambda i, h: (0, h[i]))
    outgoing = pl.pallas_call(
        pick_kernel,
        out_shape=jax.ShapeDtypeStruct((tiles * cap, rows, 2 * HEAD_DIM), jnp.bfloat16),
        grid_spec=pltpu.PrefetchScalarGridSpec(
            num_scalar_prefetch=1,
            grid=(tiles * cap,),
            in_specs=[pair, pair],
            out_specs=pl.BlockSpec((1, rows, 2 * HEAD_DIM), lambda i, h: (i, 0, 0)),
        ),
    )(heads, keys[0], values[0])
    arrived = lax.all_to_all(outgoing, "ctx", split_axis=0, concat_axis=0, tiled=True)
    own_entries = lists.reshape(HEADS * K_LIST)
    pick = own_entries * cap + entry_ranks(own_entries)
    edge = jnp.stack([me > 0, me < tiles - 1]).astype(jnp.int32)
    own = pl.BlockSpec((rows, HEAD_DIM), lambda h, p, c, e: (0, h))
    far = [
        pl.BlockSpec((1, rows, 2 * HEAD_DIM), lambda h, p, c, e, k=k: (p[h * K_LIST + k], 0, 0))
        for k in range(K_LIST)
    ]
    updated = pl.pallas_call(
        listed_kernel,
        out_shape=jax.ShapeDtypeStruct((rows, HEADS * HEAD_DIM), jnp.bfloat16),
        grid_spec=pltpu.PrefetchScalarGridSpec(
            num_scalar_prefetch=3,
            grid=(HEADS,),
            in_specs=[own] * 7 + far + [own, pl.BlockSpec((1, HEAD_DIM), lambda h, p, c, e: (0, h))],
            out_specs=own,
        ),
    )(pick, counts[0, 0], edge, queries[0], *near_k, *near_v, *([arrived] * K_LIST), residual[0], gate)
    return shifted(updated[None], "pipe", 1)


def solution(mesh):
    rows = P("pipe", "ctx", None)
    placed = (rows, rows, rows, rows, P("pipe", None), P("pipe", "ctx", None, None), rows)
    section = relay_section if mesh.shape["ctx"] == 8 else listed_section
    return jax.shard_map(section, mesh=mesh, in_specs=placed, out_specs=rows, check_vma=False)
```
